32 devices in a mesh: dp: 4 (over z), space: 8 (over y, x, core).
Axes of the slice: x: 2, y: 2, z: 4, core: 2. Of those that a mesh axis runs over, the one named last changes fastest.
Arguments:
- features: bfloat16 [4, 256, 64, 256], P('dp', 'space'), may hold values from -6 to 6
- saved: bfloat16 [3, 4, 256, 64, 256], P(None, 'dp', 'space'), may hold values from -6 to 6
- upstream: bfloat16 [3, 4, 256, 64, 256], P(None, 'dp', 'space'), may hold values from -6 to 6
- weight: bfloat16 [3, 3, 3, 256, 256], replicated, may hold values from -0.125 to 0.125
- gain: float32 [3, 256], replicated, may hold values from 0.1 to 1.9
- extent: int32 [4, 8], P('dp', 'space'), may hold values from 1 to 32, 160 in all within a row
Outputs:
- input_grad: bfloat16 [4, 256, 64, 256], P('dp', 'space')
- kernel_grad: float32 [3, 3, 3, 256, 256], replicated
The draws below stay inside these ranges and needn't reach their ends.
Inputs may be any that keep to these rules, and one draw needn't show every extreme that they name: `extent`: each scene's 8 tile extents sum to 160; some tile of each scene is wholly foreground.
All inputs are finite; a program needn't handle non-finite values. No bound on the sum of `extent` on one device may be relied on, other than what follows from the above.
Results may differ from the reference program's by a relative error of at most 0.00085.
The reference program's roundings to bfloat16 on the way (of `grad`) count: a program that leaves them out, or rounds other values in their place, can miss the bound.
Values may be sent and summed in bfloat16 or wider, within the bound.
A program may use at most 192 MiB of HBM per device.

```python
import math
import jax
import jax.numpy as jnp
import numpy as np
from jax import lax

C = 256
ROWS = 32
COLS = 64
HEIGHT = 256
SCENES = 4
N_SPACE = 8


def shard_levels(own_key, dims, cuts, smallest, high):
    level = 1.0
    for position, shards_of in cuts:
        heights = jax.random.uniform(jax.random.fold_in(jax.random.fold_in(own_key, 6), position), (shards_of,), jnp.float32, smallest / len(cuts), high / len(cuts))
        level = level * jnp.repeat(jnp.exp(heights), dims[position] // shards_of).reshape((-1,) + (1,) * (len(dims) - 1 - position))
    return level


def split_up(amount, total, bound, slope):
    weights = [(1 << 20) // math.isqrt(grade ** slope) + 1 for grade in range(2, amount + 1)]
    surplus, counts = total - bound - (amount - 1), [1] * (amount - 1)
    while surplus > 0:
        movable = [i for i in range(amount - 1) if counts[i] < bound]
        pool, remaining = sum([weights[i] for i in movable]), surplus
        for i in movable:
            addition = min(bound - counts[i], max(1, remaining * weights[i] // pool), surplus)
            counts[i] = counts[i] + addition
            surplus = surplus - addition
    return np.array([bound] + counts)


def ragged(own_key, count, total, reach, slope):
    if count == 2:
        one = jax.random.randint(own_key, (), max(1, total - reach), min(reach, total - 1) + 1)
        return jnp.stack([one, total - one])
    tallies = jnp.asarray(split_up(count, total, reach, slope), jnp.int32)
    pairs = (count - 1) // 2
    source_of, taker = tallies[1:1 + 2 * pairs:2], tallies[2:2 + 2 * pairs:2]
    room = jnp.minimum(source_of - 1, reach - taker)
    passed = jax.random.randint(jax.random.fold_in(own_key, 1), (pairs,), 0, 1 << 20) % (room + 1)
    tallies = tallies.at[1:1 + 2 * pairs:2].set(source_of - passed).at[2:2 + 2 * pairs:2].set(taker + passed)
    return tallies[jax.random.permutation(jax.random.fold_in(own_key, 2), count)]


def noise(key, shape, scale, most, shards=(), kind=jnp.bfloat16):
    entries = jax.random.normal(key, shape, jnp.float32) * scale
    if len(shards) > 0:
        entries = shard_levels(key, shape, shards, -0.22, 0.18) * entries
    return jnp.clip(entries, min=-most, max=most).astype(kind)


def setup_inputs(seed: int = 0) -> dict:
    key_of = jax.random.split(jax.random.key(seed), 7)
    features = noise(key_of[0], (SCENES, HEIGHT, COLS, C), 1.0, 6.0, ((0, 4), (1, 8)))
    saved = noise(key_of[1], (3, SCENES, HEIGHT, COLS, C), 1.0, 6.0, ((1, 4), (2, 8)))
    upstream = noise(key_of[2], (3, SCENES, HEIGHT, COLS, C), 1.0, 6.0, ((1, 4), (2, 8)))
    weight = noise(key_of[3], (3, 3, 3, C, C), (9 * C) ** -0.5, 0.125)
    gain = jnp.clip(1.0 + 0.18 * jax.random.normal(key_of[4], (3, C), jnp.float32), 0.1, 1.9)
    extent = jax.vmap(lambda own: ragged(own, N_SPACE, ROWS * 5 // 8 * N_SPACE, ROWS, 2))(jax.random.split(key_of[5], SCENES)).reshape((SCENES, N_SPACE)).astype(jnp.int32)
    return {"features": features, "saved": saved, "upstream": upstream, "weight": weight, "gain": gain, "extent": extent}


kernel_reach = 18
dilation_rates = (6, 12, 18)

def kernel_points(padded_input, dilation_step, row_total, column_total, sign_factor):
    pieces = []
    for kernel_row in range(3):
        for kernel_column in range(3):
            top_offset = kernel_reach + sign_factor * dilation_step * (kernel_row - 1)
            left_offset = kernel_reach + sign_factor * dilation_step * (kernel_column - 1)
            pieces.append(padded_input[top_offset:top_offset + row_total, left_offset:left_offset + column_total, :])
    chans = padded_input.shape[-1]
    return jnp.concatenate(pieces, axis=-1).reshape(row_total * column_total, 9 * chans)

def reference(features, saved, upstream, weight, gain, extent):
    scenes, tile_height, tile_width, chans = features.shape
    rowid = lax.iota(jnp.int32, tile_height)
    tile = rowid // ROWS
    within = rowid % ROWS
    limit = extent[:, tile]
    inside = (within[None, :] < limit).astype(jnp.float32)[:, :, None, None]
    total = jnp.sum(inside) * tile_width
    grads = []
    for b in range(3):
        values = saved[b].astype(jnp.float32)
        mean = lax.optimization_barrier(jnp.sum(values * inside, axis=(0, 1, 2))) / total
        centred = (values - mean) * inside
        variance = lax.optimization_barrier(jnp.sum(centred * centred, axis=(0, 1, 2))) / total
        rstd = 1.0 / jnp.sqrt(variance + 1e-05)
        yhat = (values - mean) * rstd
        scaled = gain[b] * upstream[b].astype(jnp.float32) * inside
        first = lax.optimization_barrier(jnp.sum(scaled, axis=(0, 1, 2)))
        second = lax.optimization_barrier(jnp.sum(scaled * yhat, axis=(0, 1, 2)))
        grad = inside * rstd * (scaled - first / total - yhat * second / total)
        grads.append(grad.astype(jnp.bfloat16))
    grads = jnp.stack(grads, axis=1)
    reversed_kernel = jnp.transpose(weight, (0, 1, 2, 4, 3)).reshape(3, 9 * chans, chans)

    def per_image(carry, items):
        image, grad_b = items
        input_padded = jnp.pad(image, ((kernel_reach, kernel_reach), (kernel_reach, kernel_reach), (0, 0)))
        output_tile = jnp.zeros((tile_height * tile_width, chans), jnp.float32)
        kernels = []
        for kernel_size in range(3):
            dilation_step = dilation_rates[kernel_size]
            gradient_padded = jnp.pad(grad_b[kernel_size], ((kernel_reach, kernel_reach), (kernel_reach, kernel_reach), (0, 0)))
            output_tile = output_tile + jnp.dot(kernel_points(gradient_padded, dilation_step, tile_height, tile_width, -1), reversed_kernel[kernel_size], preferred_element_type=jnp.float32)
            input_columns = kernel_points(input_padded, dilation_step, tile_height, tile_width, 1)
            kernels.append(lax.dot_general(input_columns, grad_b[kernel_size].reshape(tile_height * tile_width, chans), (((0,), (0,)), ((), ())), preferred_element_type=jnp.float32))
        return (carry + jnp.stack(kernels), output_tile.astype(jnp.bfloat16).reshape(tile_height, tile_width, chans))
    start = jnp.zeros((3, 9 * chans, chans), jnp.float32)
    carry, input_grad = lax.scan(per_image, start, (features, grads))
    return (input_grad, carry.reshape(3, 3, 3, chans, chans))
```

```python
import functools

import jax
import jax.numpy as jnp
from jax import lax
from jax.experimental import pallas as pl
from jax.experimental.pallas import tpu as pltpu
from jax.sharding import PartitionSpec as P

RATES = (6, 12, 18)
REACH = 18
STARTS = (0, 6, 18)
BOTH = 36
F32 = jnp.float32
BF16 = jnp.bfloat16


def local_stats(cols, ext_ref, saved_ref, up_ref, gain_ref, out_ref):
    limit = ext_ref[0, 0]
    chans = saved_ref.shape[-1]
    pivot = saved_ref[0, 0:16, :].astype(F32)[0:1]

    def fold(x):
        return jnp.sum(x.reshape(cols // 8, 8, chans), axis=0)

    def step(h, carry):
        at = pl.ds(pl.multiple_of(h * cols, cols), cols)
        d = saved_ref[0, at, :].astype(F32) - pivot
        u = up_ref[0, at, :].astype(F32)
        a, b, c, e = carry
        return (a + fold(d), b + fold(d * d), c + fold(u), e + fold(u * d))

    zero = jnp.zeros((8, chans), F32)
    sums = lax.fori_loop(0, limit, step, (zero, zero, zero, zero))
    d, dd, u, ud = [jnp.sum(x, axis=0, keepdims=True) for x in sums]
    n = jnp.full((1, chans), limit * cols, jnp.int32).astype(F32)
    off = d / n
    gain = gain_ref[...]
    rows = [n * pivot + d, dd - d * off, gain * u, gain * (ud - u * off), n]
    out_ref[...] = jnp.concatenate(rows + [jnp.zeros((3, chans), F32)], axis=0)


def merge(parts):
    n = sum(p[4:5] for p in parts)
    mean = sum(p[0:1] for p in parts) / n
    m2 = jnp.zeros_like(n)
    cross = jnp.zeros_like(n)
    for p in parts:
        gap = p[0:1] / p[4:5] - mean
        m2 = m2 + p[1:2] + p[4:5] * gap * gap
        cross = cross + p[3:4] + p[2:3] * gap
    return mean, n, m2, sum(p[2:3] for p in parts), cross


def exchange(sizes, st_ref, gain_ref, out_ref, buf_a, buf_b, mid, send_a, recv_a, send_b, recv_b):
    barrier = pltpu.get_barrier_semaphore()
    for axis, count in sizes:
        me = lax.axis_index(axis)
        for k in range(1, count):
            pl.semaphore_signal(
                barrier, inc=1, device_id={axis: lax.rem(me + k, count)},
                device_id_type=pl.DeviceIdType.MESH,
            )
    pl.semaphore_wait(barrier, sum(count - 1 for _, count in sizes))

    def spread(axis, count, src, buf, send, recv):
        me = lax.axis_index(axis)
        copies = []
        for k in range(1, count):
            copies.append(pltpu.make_async_remote_copy(
                src_ref=src, dst_ref=buf.at[k - 1], send_sem=send.at[k - 1], recv_sem=recv.at[k - 1],
                device_id={axis: lax.rem(me + k, count)}, device_id_type=pl.DeviceIdType.MESH,
            ))
        for copy in copies:
            copy.start()
        for copy in copies:
            copy.wait()
        return merge([src[...]] + [buf[k] for k in range(count - 1)])

    mean, n, m2, s1, cross = spread(*sizes[0], st_ref, buf_a, send_a, recv_a)
    pad = jnp.zeros((3, n.shape[1]), F32)
    mid[...] = jnp.concatenate([mean * n, m2, s1, cross, n, pad], axis=0)
    mean, n, m2, s1, cross = spread(*sizes[1], mid, buf_b, send_b, recv_b)
    rstd = 1.0 / jnp.sqrt(m2 / n + 1e-05)
    slope = rstd * (rstd * (rstd * cross / n))
    rows = [gain_ref[...] * rstd, slope, rstd * (s1 / n), mean]
    out_ref[...] = jnp.concatenate(rows + [jnp.zeros((4, n.shape[1]), F32)], axis=0)


def shifted(g, dx, cols):
    if dx == 0:
        return g
    w = lax.broadcasted_iota(jnp.int32, g.shape, 0)
    keep = (w >= dx) if dx > 0 else (w < cols + dx)
    return jnp.where(keep, pltpu.roll(g, dx % cols, axis=0), 0.0)


def gradients(cols, rows, ext_ref, saved_ref, up_ref, coef_ref, out_ref, top_ref, bottom_ref):
    limit = ext_ref[0, 0]
    branch = pl.program_id(0)
    coef = coef_ref[...]
    a, b, c, mean = coef[0:1], coef[1:2], coef[2:3], coef[3:4]
    for k, rate in enumerate(RATES):

        @pl.when(branch == k)
        def _():
            def step(h, _):
                at = pl.ds(pl.multiple_of(h * cols, cols), cols)
                v = saved_ref[0, at, :].astype(F32)
                u = up_ref[0, at, :].astype(F32)
                g = a * u - c - b * (v - mean)
                g = jnp.where(h < limit, g, 0.0)
                for j in range(3):
                    out_ref[0, j, at, :] = shifted(g, rate * (j - 1), cols).astype(BF16)
                return 0

            lax.fori_loop(0, rows, step, 0)
            here = pl.ds(STARTS[k] * cols, rate * cols)
            top_ref[here, :] = out_ref[0, 1, 0 : rate * cols, :]
            bottom_ref[here, :] = out_ref[0, 1, (rows - rate) * cols : rows * cols, :]


def kernel_terms(cols, rows, before_ref, own_ref, after_ref, g_ref, out_ref, ft):
    branch, column = pl.program_id(0), pl.program_id(1)

    @pl.when((branch == 0) & (column == 0))
    def _():
        start = 0
        for ref in (before_ref, own_ref, after_ref):
            for k in range(ref.shape[0] // 128):
                ft[:, start : start + 128] = ref[k * 128 : (k + 1) * 128, :].T
                start += 128

    rate = 6 * (branch + 1)
    parts = []
    for i in range(3):
        at = pl.multiple_of((REACH + rate * (i - 1)) * cols, 128)
        parts.append(ft[:, pl.ds(at, rows * cols)])
    got = jnp.dot(jnp.concatenate(parts, axis=0), g_ref[0, 0], preferred_element_type=F32)
    out_ref[0, :, 0] = got.reshape(out_ref.shape[1], out_ref.shape[3], out_ref.shape[4])


def input_terms(cols, rows, before_ref, after_ref, g_ref, w_ref, out_ref, ext, acc):
    branch, column = pl.program_id(0), pl.program_id(1)
    ext[REACH * cols : (REACH + rows) * cols, :] = g_ref[0, 0]
    for k, rate in enumerate(RATES):
        for j in range(3):

            @pl.when((branch == k) & (column == j))
            def _():
                def step(r, _):
                    src = pl.ds(pl.multiple_of((STARTS[k] + r) * cols, cols), cols)
                    up = pl.ds(pl.multiple_of((REACH - rate + r) * cols, cols), cols)
                    down = pl.ds(pl.multiple_of((REACH + rows + r) * cols, cols), cols)
                    dx = rate * (j - 1)
                    ext[up, :] = shifted(before_ref[src, :].astype(F32), dx, cols).astype(BF16)
                    ext[down, :] = shifted(after_ref[src, :].astype(F32), dx, cols).astype(BF16)
                    return 0

                lax.fori_loop(0, rate, step, 0)

    rate = 6 * (branch + 1)
    first = (branch == 0) & (column == 0)
    last = (branch == 2) & (column == 2)
    tile = 512

    def block(m, _):
        here = pl.ds(pl.multiple_of(m * tile, tile), tile)
        total = jnp.where(first, 0.0, acc[here, :])
        for i in range(3):
            at = pl.multiple_of((REACH - rate * (i - 1)) * cols + m * tile, cols)
            total = total + lax.dot_general(
                ext[pl.ds(at, tile), :], w_ref[0, i, 0], (((1,), (1,)), ((), ())),
                preferred_element_type=F32,
            )
        acc[here, :] = total

        @pl.when(last)
        def _():
            out_ref[here, :] = total.astype(BF16)

        return 0

    lax.fori_loop(0, rows * cols // tile, block, 0)


def vmem(shape=None, index=None):
    if shape is None:
        return pl.BlockSpec(memory_space=pltpu.VMEM)
    return pl.BlockSpec(shape, index)


def body(features, saved, upstream, weight, gain, extent):
    rows, cols, chans = features.shape[1:]
    pixels = rows * cols
    n_space, n_dp = lax.axis_size("space"), lax.axis_size("dp")
    smem = pl.BlockSpec(memory_space=pltpu.SMEM)
    limit = pltpu.CompilerParams(vmem_limit_bytes=60 * 1024 * 1024)

    feats = features.reshape(pixels, chans)
    up_pairs = [(i, i + 1) for i in range(n_space - 1)]
    down_pairs = [(j, i) for i, j in up_pairs]
    f_before = lax.ppermute(feats[pixels - REACH * cols :], "space", up_pairs)
    f_after = lax.ppermute(feats[: REACH * cols], "space", down_pairs)

    s = saved.reshape(3, pixels, chans)
    u = upstream.reshape(3, pixels, chans)
    wide = gain.reshape(1, 3 * chans)
    stats = pl.pallas_call(
        functools.partial(local_stats, cols),
        grid=(3,),
        in_specs=[
            smem,
            vmem((1, pixels, chans), lambda b: (b, 0, 0)),
            vmem((1, pixels, chans), lambda b: (b, 0, 0)),
            vmem((1, chans), lambda b: (0, b)),
        ],
        out_specs=vmem((8, chans), lambda b: (0, b)),
        out_shape=jax.ShapeDtypeStruct((8, 3 * chans), F32),
        compiler_params=limit,
    )(extent, s, u, wide)
    coef = pl.pallas_call(
        functools.partial(exchange, (("space", n_space), ("dp", n_dp))),
        in_specs=[vmem(), vmem()],
        out_specs=vmem(),
        out_shape=jax.ShapeDtypeStruct((8, 3 * chans), F32),
        scratch_shapes=[
            pltpu.VMEM((n_space - 1, 8, 3 * chans), F32),
            pltpu.VMEM((n_dp - 1, 8, 3 * chans), F32),
            pltpu.VMEM((8, 3 * chans), F32),
            pltpu.SemaphoreType.DMA((n_space - 1,)),
            pltpu.SemaphoreType.DMA((n_space - 1,)),
            pltpu.SemaphoreType.DMA((n_dp - 1,)),
            pltpu.SemaphoreType.DMA((n_dp - 1,)),
        ],
        compiler_params=pltpu.CompilerParams(collective_id=0, has_side_effects=True),
    )(stats, wide)
    halo = jax.ShapeDtypeStruct((BOTH * cols, chans), BF16)
    grads, top, bottom = pl.pallas_call(
        functools.partial(gradients, cols, rows),
        grid=(3,),
        in_specs=[
            smem,
            vmem((1, pixels, chans), lambda b: (b, 0, 0)),
            vmem((1, pixels, chans), lambda b: (b, 0, 0)),
            vmem((8, chans), lambda b: (0, b)),
        ],
        out_specs=[
            vmem((1, 3, pixels, chans), lambda b: (b, 0, 0, 0)),
            vmem((BOTH * cols, chans), lambda b: (0, 0)),
            vmem((BOTH * cols, chans), lambda b: (0, 0)),
        ],
        out_shape=[jax.ShapeDtypeStruct((3, 3, pixels, chans), BF16), halo, halo],
        compiler_params=limit,
    )(extent, s, u, coef)
    g_before = lax.ppermute(bottom, "space", up_pairs)
    g_after = lax.ppermute(top, "space", down_pairs)
    flops = 2 * 27 * pixels * chans * chans
    cost = pl.CostEstimate(flops=flops, bytes_accessed=20_000_000, transcendentals=0)
    terms = pl.pallas_call(
        functools.partial(kernel_terms, cols, rows),
        grid=(3, 3),
        in_specs=[
            vmem((REACH * cols, chans), lambda b, j: (0, 0)),
            vmem((pixels, chans), lambda b, j: (0, 0)),
            vmem((REACH * cols, chans), lambda b, j: (0, 0)),
            vmem((1, 1, pixels, chans), lambda b, j: (b, j, 0, 0)),
        ],
        out_specs=vmem((1, 3, 1, chans, chans), lambda b, j: (b, 0, j, 0, 0)),
        out_shape=jax.ShapeDtypeStruct((3, 3, 3, chans, chans), F32),
        scratch_shapes=[pltpu.VMEM((chans, pixels + BOTH * cols), BF16)],
        compiler_params=limit,
        cost_estimate=cost,
    )(f_before, feats, f_after, grads)
    kernel_grad = lax.psum(terms, ("dp", "space"))
    out = pl.pallas_call(
        functools.partial(input_terms, cols, rows),
        grid=(3, 3),
        in_specs=[
            vmem((BOTH * cols, chans), lambda b, j: (0, 0)),
            vmem((BOTH * cols, chans), lambda b, j: (0, 0)),
            vmem((1, 1, pixels, chans), lambda b, j: (b, j, 0, 0)),
            vmem((1, 3, 1, chans, chans), lambda b, j: (b, 0, j, 0, 0)),
        ],
        out_specs=vmem((pixels, chans), lambda b, j: (0, 0)),
        out_shape=jax.ShapeDtypeStruct((pixels, chans), BF16),
        scratch_shapes=[
            pltpu.VMEM((pixels + BOTH * cols, chans), BF16),
            pltpu.VMEM((pixels, chans), F32),
        ],
        compiler_params=limit,
        cost_estimate=cost,
    )(g_before, g_after, grads, weight)
    return out.reshape(1, rows, cols, chans), kernel_grad


def solution(mesh):
    return jax.shard_map(
        body,
        mesh=mesh,
        in_specs=(
            P("dp", "space", None, None),
            P(None, "dp", "space", None, None),
            P(None, "dp", "space", None, None),
            P(),
            P(),
            P("dp", "space"),
        ),
        out_specs=(P("dp", "space", None, None), P()),
        check_vma=False,
    )
```

```python
import functools

import jax
import jax.numpy as jnp
from jax import lax
from jax.experimental import pallas as pl
from jax.experimental.pallas import tpu as pltpu
from jax.sharding import PartitionSpec as P

RATES = (6, 12, 18)
REACH = 18
STARTS = (0, 6, 18)
BOTH = 36
F32 = jnp.float32
BF16 = jnp.bfloat16


def local_stats(cols, ext_ref, saved_ref, up_ref, gain_ref, out_ref):
    limit = ext_ref[0, 0]
    chans = saved_ref.shape[-1]
    pivot = saved_ref[0, 0:16, :].astype(F32)[0:1]

    def fold(x):
        return jnp.sum(x.reshape(cols // 8, 8, chans), axis=0)

    def step(h, carry):
        at = pl.ds(pl.multiple_of(h * cols, cols), cols)
        d = saved_ref[0, at, :].astype(F32) - pivot
        u = up_ref[0, at, :].astype(F32)
        a, b, c, e = carry
        return (a + fold(d), b + fold(d * d), c + fold(u), e + fold(u * d))

    zero = jnp.zeros((8, chans), F32)
    sums = lax.fori_loop(0, limit, step, (zero, zero, zero, zero))
    d, dd, u, ud = [jnp.sum(x, axis=0, keepdims=True) for x in sums]
    n = jnp.full((1, chans), limit * cols, jnp.int32).astype(F32)
    off = d / n
    gain = gain_ref[...]
    rows = [n * pivot + d, dd - d * off, gain * u, gain * (ud - u * off), n]
    out_ref[...] = jnp.concatenate(rows + [jnp.zeros((3, chans), F32)], axis=0)


def merge(parts):
    n = sum(p[4:5] for p in parts)
    mean = sum(p[0:1] for p in parts) / n
    m2 = jnp.zeros_like(n)
    cross = jnp.zeros_like(n)
    for p in parts:
        gap = p[0:1] / p[4:5] - mean
        m2 = m2 + p[1:2] + p[4:5] * gap * gap
        cross = cross + p[3:4] + p[2:3] * gap
    return mean, n, m2, sum(p[2:3] for p in parts), cross


def exchange(sizes, st_ref, gain_ref, out_ref, buf_a, buf_b, mid, send_a, recv_a, send_b, recv_b):
    barrier = pltpu.get_barrier_semaphore()
    for axis, count in sizes:
        me = lax.axis_index(axis)
        for k in range(1, count):
            pl.semaphore_signal(
                barrier, inc=1, device_id={axis: lax.rem(me + k, count)},
                device_id_type=pl.DeviceIdType.MESH,
            )
    pl.semaphore_wait(barrier, sum(count - 1 for _, count in sizes))

    def spread(axis, count, src, buf, send, recv):
        me = lax.axis_index(axis)
        copies = []
        for k in range(1, count):
            copies.append(pltpu.make_async_remote_copy(
                src_ref=src, dst_ref=buf.at[k - 1], send_sem=send.at[k - 1], recv_sem=recv.at[k - 1],
                device_id={axis: lax.rem(me + k, count)}, device_id_type=pl.DeviceIdType.MESH,
            ))
        for copy in copies:
            copy.start()
        for copy in copies:
            copy.wait()
        return merge([src[...]] + [buf[k] for k in range(count - 1)])

    mean, n, m2, s1, cross = spread(*sizes[0], st_ref, buf_a, send_a, recv_a)
    pad = jnp.zeros((3, n.shape[1]), F32)
    mid[...] = jnp.concatenate([mean * n, m2, s1, cross, n, pad], axis=0)
    mean, n, m2, s1, cross = spread(*sizes[1], mid, buf_b, send_b, recv_b)
    rstd = 1.0 / jnp.sqrt(m2 / n + 1e-05)
    slope = rstd * (rstd * (rstd * cross / n))
    rows = [gain_ref[...] * rstd, slope, rstd * (s1 / n), mean]
    out_ref[...] = jnp.concatenate(rows + [jnp.zeros((4, n.shape[1]), F32)], axis=0)


def shifted(g, dx, cols):
    if dx == 0:
        return g
    w = lax.broadcasted_iota(jnp.int32, g.shape, 0)
    keep = (w >= dx) if dx > 0 else (w < cols + dx)
    return jnp.where(keep, pltpu.roll(g, dx % cols, axis=0), 0.0)


def gradients(cols, rows, ext_ref, saved_ref, up_ref, coef_ref, out_ref, top_ref, bottom_ref):
    limit = ext_ref[0, 0]
    branch = pl.program_id(0)
    coef = coef_ref[...]
    a, b, c, mean = coef[0:1], coef[1:2], coef[2:3], coef[3:4]
    for k, rate in enumerate(RATES):

        @pl.when(branch == k)
        def _():
            def step(h, _):
                at = pl.ds(pl.multiple_of(h * cols, cols), cols)
                v = saved_ref[0, at, :].astype(F32)
                u = up_ref[0, at, :].astype(F32)
                g = a * u - c - b * (v - mean)
                g = jnp.where(h < limit, g, 0.0)
                for j in range(3):
                    out_ref[0, j, at, :] = shifted(g, rate * (j - 1), cols).astype(BF16)
                return 0

            lax.fori_loop(0, rows, step, 0)
            here = pl.ds(STARTS[k] * cols, rate * cols)
            top_ref[here, :] = out_ref[0, 1, 0 : rate * cols, :]
            bottom_ref[here, :] = out_ref[0, 1, (rows - rate) * cols : rows * cols, :]


def kernel_terms(cols, rows, before_ref, own_ref, after_ref, g_ref, out_ref, ft):
    branch, column = pl.program_id(0), pl.program_id(1)

    @pl.when((branch == 0) & (column == 0))
    def _():
        start = 0
        for ref in (before_ref, own_ref, after_ref):
            for k in range(ref.shape[0] // 128):
                ft[:, start : start + 128] = ref[k * 128 : (k + 1) * 128, :].T
                start += 128

    rate = 6 * (branch + 1)
    parts = []
    for i in range(3):
        at = pl.multiple_of((REACH + rate * (i - 1)) * cols, 128)
        parts.append(ft[:, pl.ds(at, rows * cols)])
    got = jnp.dot(jnp.concatenate(parts, axis=0), g_ref[0, 0], preferred_element_type=F32)
    out_ref[0, :, 0] = got.reshape(out_ref.shape[1], out_ref.shape[3], out_ref.shape[4])


def input_terms(cols, rows, before_ref, after_ref, g_ref, w_ref, k_ref, out_ref, k_out, ext, acc):
    branch, column = pl.program_id(0), pl.program_id(1)
    k_out[...] = k_ref[...]
    ext[REACH * cols : (REACH + rows) * cols, :] = g_ref[0, 0]
    for k, rate in enumerate(RATES):
        for j in range(3):

            @pl.when((branch == k) & (column == j))
            def _():
                def step(r, _):
                    src = pl.ds(pl.multiple_of((STARTS[k] + r) * cols, cols), cols)
                    up = pl.ds(pl.multiple_of((REACH - rate + r) * cols, cols), cols)
                    down = pl.ds(pl.multiple_of((REACH + rows + r) * cols, cols), cols)
                    dx = rate * (j - 1)
                    ext[up, :] = shifted(before_ref[src, :].astype(F32), dx, cols).astype(BF16)
                    ext[down, :] = shifted(after_ref[src, :].astype(F32), dx, cols).astype(BF16)
                    return 0

                lax.fori_loop(0, rate, step, 0)

    rate = 6 * (branch + 1)
    first = (branch == 0) & (column == 0)
    last = (branch == 2) & (column == 2)
    tile = 512

    def block(m, _):
        here = pl.ds(pl.multiple_of(m * tile, tile), tile)
        total = jnp.where(first, 0.0, acc[here, :])
        for i in range(3):
            at = pl.multiple_of((REACH - rate * (i - 1)) * cols + m * tile, cols)
            total = total + lax.dot_general(
                ext[pl.ds(at, tile), :], w_ref[0, i, 0], (((1,), (1,)), ((), ())),
                preferred_element_type=F32,
            )
        acc[here, :] = total

        @pl.when(last)
        def _():
            out_ref[here, :] = total.astype(BF16)

        return 0

    lax.fori_loop(0, rows * cols // tile, block, 0)


def reduce_all(n_space, n_dp, in_ref, out_ref, acc, rb, send, recv):
    bits = n_space.bit_length() - 1
    pieces = n_space * n_dp
    streams = in_ref.shape[0]
    space, dp = lax.axis_index("space"), lax.axis_index("dp")
    mesh_id = pl.DeviceIdType.MESH

    def bit_of(b):
        return lax.rem(lax.div(space, 1 << b), 2)

    def partner(b):
        return {"space": space + (1 - 2 * bit_of(b)) * (1 << b)}

    def peer(k):
        return {"dp": lax.rem(dp + k, n_dp)}

    others = [partner(b) for b in range(bits)] + [peer(k) for k in range(1, n_dp)]
    barrier = pltpu.get_barrier_semaphore()
    for other in others:
        pl.semaphore_signal(barrier, inc=1, device_id=other, device_id_type=mesh_id)
    pl.semaphore_wait(barrier, len(others))

    def stages(st):
        order = list(range(bits)) if st % 2 == 0 else [0] + list(range(bits - 1, 0, -1))
        sem = 0

        def copy(src, dst, k, device):
            c = pltpu.make_async_remote_copy(
                src_ref=src, dst_ref=dst, send_sem=send.at[st, k], recv_sem=recv.at[st, k],
                device_id=device, device_id_type=mesh_id,
            )
            c.start()
            return c

        starts = []
        base, room, size = 0, 0, pieces
        for level, b in enumerate(order):
            size = size // 2
            mine = bit_of(b)
            here, there = base + mine * size, base + (1 - mine) * size
            src = in_ref if level == 0 else acc
            c = copy(src.at[st, pl.ds(there, size)], rb.at[st, pl.ds(room, size)], sem, partner(b))
            sem += 1
            yield
            c.wait()
            dst = 0 if level == 0 else here

            def add(i, _, src=src, here=here, dst=dst, room=room):
                acc[st, dst + i] = src[st, here + i] + rb[st, room + i]
                return 0

            lax.fori_loop(0, size, add, 0)
            starts.append((mine, size))
            base = dst
            room += size
        whole = 0
        ranges = []
        for mine, size in starts:
            whole = whole + mine * size
            ranges.append((whole, size))
        copies = []
        for k in range(1, n_dp):
            to = lax.rem(dp + k, n_dp)
            copies.append(copy(acc.at[st, base + to], rb.at[st, room + k - 1], sem, peer(k)))
            sem += 1
        yield
        total = acc[st, base + dp]
        for k in range(1, n_dp):
            copies[k - 1].wait()
            total = total + rb[st, room + k - 1]
        out_ref[st, whole + dp] = total
        copies = []
        for k in range(1, n_dp):
            copies.append(copy(out_ref.at[st, whole + dp], out_ref.at[st, whole + dp], sem, peer(k)))
            sem += 1
        yield
        for c in copies:
            c.wait()
        for (start, size), b in zip(ranges[::-1], order[::-1]):
            span = out_ref.at[st, pl.ds(start, size)]
            c = copy(span, span, sem, partner(b))
            sem += 1
            yield
            c.wait()

    running = []
    waiting = [stages(st) for st in range(streams)]
    while running or waiting:
        alive = []
        for run in running:
            if next(run, 0) is None:
                alive.append(run)
        running = alive
        if waiting:
            run = waiting.pop(0)
            next(run)
            running.append(run)


def vmem(shape=None, index=None):
    if shape is None:
        return pl.BlockSpec(memory_space=pltpu.VMEM)
    return pl.BlockSpec(shape, index)


def body(features, saved, upstream, weight, gain, extent):
    rows, cols, chans = features.shape[1:]
    pixels = rows * cols
    n_space, n_dp = lax.axis_size("space"), lax.axis_size("dp")
    smem = pl.BlockSpec(memory_space=pltpu.SMEM)
    limit = pltpu.CompilerParams(vmem_limit_bytes=60 * 1024 * 1024)

    feats = features.reshape(pixels, chans)
    up_pairs = [(i, i + 1) for i in range(n_space - 1)]
    down_pairs = [(j, i) for i, j in up_pairs]
    f_before = lax.ppermute(feats[pixels - REACH * cols :], "space", up_pairs)
    f_after = lax.ppermute(feats[: REACH * cols], "space", down_pairs)

    s = saved.reshape(3, pixels, chans)
    u = upstream.reshape(3, pixels, chans)
    wide = gain.reshape(1, 3 * chans)
    stats = pl.pallas_call(
        functools.partial(local_stats, cols),
        grid=(3,),
        in_specs=[
            smem,
            vmem((1, pixels, chans), lambda b: (b, 0, 0)),
            vmem((1, pixels, chans), lambda b: (b, 0, 0)),
            vmem((1, chans), lambda b: (0, b)),
        ],
        out_specs=vmem((8, chans), lambda b: (0, b)),
        out_shape=jax.ShapeDtypeStruct((8, 3 * chans), F32),
        compiler_params=limit,
    )(extent, s, u, wide)
    coef = pl.pallas_call(
        functools.partial(exchange, (("space", n_space), ("dp", n_dp))),
        in_specs=[vmem(), vmem()],
        out_specs=vmem(),
        out_shape=jax.ShapeDtypeStruct((8, 3 * chans), F32),
        scratch_shapes=[
            pltpu.VMEM((n_space - 1, 8, 3 * chans), F32),
            pltpu.VMEM((n_dp - 1, 8, 3 * chans), F32),
            pltpu.VMEM((8, 3 * chans), F32),
            pltpu.SemaphoreType.DMA((n_space - 1,)),
            pltpu.SemaphoreType.DMA((n_space - 1,)),
            pltpu.SemaphoreType.DMA((n_dp - 1,)),
            pltpu.SemaphoreType.DMA((n_dp - 1,)),
        ],
        compiler_params=pltpu.CompilerParams(collective_id=0, has_side_effects=True),
    )(stats, wide)
    halo = jax.ShapeDtypeStruct((BOTH * cols, chans), BF16)
    grads, top, bottom = pl.pallas_call(
        functools.partial(gradients, cols, rows),
        grid=(3,),
        in_specs=[
            smem,
            vmem((1, pixels, chans), lambda b: (b, 0, 0)),
            vmem((1, pixels, chans), lambda b: (b, 0, 0)),
            vmem((8, chans), lambda b: (0, b)),
        ],
        out_specs=[
            vmem((1, 3, pixels, chans), lambda b: (b, 0, 0, 0)),
            vmem((BOTH * cols, chans), lambda b: (0, 0)),
            vmem((BOTH * cols, chans), lambda b: (0, 0)),
        ],
        out_shape=[jax.ShapeDtypeStruct((3, 3, pixels, chans), BF16), halo, halo],
        compiler_params=limit,
    )(extent, s, u, coef)
    g_before = lax.ppermute(bottom, "space", up_pairs)
    g_after = lax.ppermute(top, "space", down_pairs)
    flops = 2 * 27 * pixels * chans * chans
    cost = pl.CostEstimate(flops=flops, bytes_accessed=20_000_000, transcendentals=0)
    terms = pl.pallas_call(
        functools.partial(kernel_terms, cols, rows),
        grid=(3, 3),
        in_specs=[
            vmem((REACH * cols, chans), lambda b, j: (0, 0)),
            vmem((pixels, chans), lambda b, j: (0, 0)),
            vmem((REACH * cols, chans), lambda b, j: (0, 0)),
            vmem((1, 1, pixels, chans), lambda b, j: (b, j, 0, 0)),
        ],
        out_specs=vmem((1, 3, 1, chans, chans), lambda b, j: (b, 0, j, 0, 0)),
        out_shape=jax.ShapeDtypeStruct((3, 3, 3, chans, chans), F32),
        scratch_shapes=[pltpu.VMEM((chans, pixels + BOTH * cols), BF16)],
        compiler_params=limit,
        cost_estimate=cost,
    )(f_before, feats, f_after, grads)
    streams, pieces = 9, n_space * n_dp
    per = 27 * chans // (streams * pieces)
    shape = (streams, pieces, per, chans)
    room = pieces - n_dp + n_dp - 1
    sems = pltpu.SemaphoreType.DMA((streams, 2 * (n_space.bit_length() - 1 + n_dp - 1)))
    reduced = pl.pallas_call(
        functools.partial(reduce_all, n_space, n_dp),
        in_specs=[vmem()],
        out_specs=vmem(),
        out_shape=jax.ShapeDtypeStruct(shape, F32),
        scratch_shapes=[
            pltpu.VMEM((streams, pieces // 2, per, chans), F32),
            pltpu.VMEM((streams, room, per, chans), F32),
            sems,
            sems,
        ],
        compiler_params=pltpu.CompilerParams(
            collective_id=1, has_side_effects=True, vmem_limit_bytes=60 * 1024 * 1024
        ),
    )(terms.reshape(shape)).reshape(streams, 3 * chans, chans)
    out, kernel_grad = pl.pallas_call(
        functools.partial(input_terms, cols, rows),
        grid=(3, 3),
        in_specs=[
            vmem((BOTH * cols, chans), lambda b, j: (0, 0)),
            vmem((BOTH * cols, chans), lambda b, j: (0, 0)),
            vmem((1, 1, pixels, chans), lambda b, j: (b, j, 0, 0)),
            vmem((1, 3, 1, chans, chans), lambda b, j: (b, 0, j, 0, 0)),
            vmem((1, 3 * chans, chans), lambda b, j: (3 * b + j, 0, 0)),
        ],
        out_specs=[
            vmem((pixels, chans), lambda b, j: (0, 0)),
            vmem((1, 3 * chans, chans), lambda b, j: (3 * b + j, 0, 0)),
        ],
        out_shape=[
            jax.ShapeDtypeStruct((pixels, chans), BF16),
            jax.ShapeDtypeStruct((streams, 3 * chans, chans), F32),
        ],
        scratch_shapes=[
            pltpu.VMEM((pixels + BOTH * cols, chans), BF16),
            pltpu.VMEM((pixels, chans), F32),
        ],
        compiler_params=limit,
        cost_estimate=cost,
    )(g_before, g_after, grads, weight, reduced)
    return out.reshape(1, rows, cols, chans), kernel_grad.reshape(weight.shape)


def solution(mesh):
    return jax.shard_map(
        body,
        mesh=mesh,
        in_specs=(
            P("dp", "space", None, None),
            P(None, "dp", "space", None, None),
            P(None, "dp", "space", None, None),
            P(),
            P(),
            P("dp", "space"),
        ),
        out_specs=(P("dp", "space", None, None), P()),
        check_vma=False,
    )
```
